32 devices in a mesh: freq: 4 (over y, core), space: 8 (over z, x).
Axes of the slice: x: 2, y: 2, z: 4, core: 2. Of those that a mesh axis runs over, the one named last changes fastest.
Arguments:
- traces: float32 [1024, 512, 256], P(('freq', 'space')), may hold values from -50 to 50
- probes: float32 [8, 128, 64], P('freq'), may hold values from -0.5 to 0.5
Outputs:
- denoised: float32 [1024, 512, 256], P(('freq', 'space'))
The draws below stay inside these ranges and needn't reach their ends.
All inputs are finite; a program needn't handle non-finite values.
Results may differ from the reference program's by a relative error of at most 0.000092.
Values sent between devices are 32-bit elements; how exact they have to be, the bound alone decides.
No kernel may reach another device: no remote copies, remote signals or barrier semaphores. Data moves between devices by JAX's collectives and lax.ppermute only.
A program may use at most 192 MiB of HBM per device.

```python
import jax
import jax.numpy as jnp
from jax import lax

NT = 1024
NX = 256
NY = 512
RANK = 64
BAND_LO = 16
NF = 8
COLUMNS = 128


def draw_traces(key, part):
    subkeys = jax.random.split(key, 4)
    noise_field = jnp.clip(jax.random.normal(subkeys[0], (NT, NY, NX), jnp.float32), -6.0, 6.0)
    inline_gain = jnp.exp(jax.random.uniform(subkeys[1], (NX,), jnp.float32, jnp.log(0.5), jnp.log(2.0)))
    rising = 3.0 ** (jnp.arange(NY, dtype=jnp.float32) / max(NY - 1, 1) - 0.5)
    cross_gain = jnp.exp(jax.random.uniform(subkeys[2], (NY,), jnp.float32, jnp.log(0.5), jnp.log(2.0))) * rising
    result = noise_field * cross_gain[None, :, None] * inline_gain[None, None, :]
    params = jax.random.uniform(subkeys[3], (4, 5), jnp.float32)
    sample_times = jnp.arange(NT, dtype=jnp.float32)[:, None, None]
    inline_axis = jnp.arange(NX, dtype=jnp.float32)[None, None, :]
    cross_axis = jnp.arange(NY, dtype=jnp.float32)[None, :, None]
    for event_index in range(4):
        onset_time = params[event_index, 0] * NT
        dip_inline = (params[event_index, 1] - 0.5) * 0.5
        dip_cross = (params[event_index, 2] - 0.5) * 0.5
        amplitude = 0.5 + params[event_index, 3]
        delay_field = sample_times - onset_time - dip_inline * inline_axis - dip_cross * cross_axis
        delay_field = jnp.mod(delay_field + NT / 2.0, NT) - NT / 2.0
        ricker_arg = (jnp.pi * (0.02 + 0.02 * params[event_index, 4]) * delay_field) ** 2
        result = result + amplitude * (1.0 - 2.0 * ricker_arg) * jnp.exp(-ricker_arg)
    return result


def block_scale(stream_key, dims, cuts, smallest, high):
    loudness = 1.0
    for dim, blocks in cuts:
        draws = jax.random.uniform(jax.random.fold_in(jax.random.fold_in(stream_key, 6), dim), (blocks,), jnp.float32, smallest / len(cuts), high / len(cuts))
        loudness = loudness * jnp.repeat(jnp.exp(draws), dims[dim] // blocks).reshape((-1,) + (1,) * (len(dims) - 1 - dim))
    return loudness


def noise(key, shape, deviation, reach, shards=(), kind=jnp.bfloat16):
    array = deviation * jax.random.normal(key, shape, jnp.float32)
    if shards:
        array = array * block_scale(key, shape, shards, -0.22, 0.18)
    return jnp.clip(array, -reach, reach).astype(kind)


def setup_inputs(seed: int = 0) -> dict:
    seeds = jax.random.split(jax.random.key(seed), 3)
    traces = draw_traces(jax.random.fold_in(seeds[2], 71), 0)
    probes = noise(seeds[1], (NF, COLUMNS, RANK), COLUMNS ** -0.5, 0.5, ((0, 4),), jnp.float32)
    return {"traces": traces, "probes": probes}


HIGHEST_PRECISION = lax.Precision.HIGHEST

def wave_table(freq_ids, time_ids, period, factor):
    phase = (freq_ids[:, None] * time_ids[None, :] % period).astype(jnp.float32) * (2.0 * jnp.pi / period)
    return jnp.stack([jnp.cos(phase), -jnp.sin(phase)]) * factor

def hankel(spectrum, window, columns):
    width = spectrum.shape[-1]
    tiled = jnp.tile(spectrum, (1, 1, window + 1))[:, :, :window * (width + 1)]
    return tiled.reshape(spectrum.shape[0], spectrum.shape[1], window, width + 1)[:, :, :, :columns]

def diag_mean(blocks, width):
    halves, channels, window, columns = blocks.shape
    padded = jnp.pad(blocks, ((0, 0), (0, 0), (0, 0), (0, width + 1 - columns)))
    flat_rows = padded.reshape(halves, channels, window * (width + 1))
    flat_rows = jnp.pad(flat_rows, ((0, 0), (0, 0), (0, width - window)))
    totals = flat_rows.reshape(halves, channels, window + 1, width).sum(axis=2)
    position = jnp.arange(width, dtype=jnp.int32)
    counts = jnp.minimum(jnp.minimum(position + 1, width - position), min(window, columns))
    return totals / counts.astype(jnp.float32)

def assemble(gram_raw, cross_raw):
    half = gram_raw.shape[-1] // 2
    diagonal_part = gram_raw[..., :half, :half] + gram_raw[..., half:, half:]
    skew_part = gram_raw[..., half:, :half] - gram_raw[..., :half, half:]
    gram_matrix = jnp.concatenate([jnp.concatenate([diagonal_part, skew_part], -1), jnp.concatenate([-skew_part, diagonal_part], -1)], -2)
    real_rows = cross_raw[..., 0, :, :]
    imag_rows = cross_raw[..., 1, :, :]
    cross_terms = jnp.concatenate([real_rows[..., :half, :] + imag_rows[..., half:, :], imag_rows[..., :half, :] - real_rows[..., half:, :]], -2)
    return (gram_matrix, cross_terms)

def denoise_slice(slice_pair):
    spectrum, probe = slice_pair
    width = spectrum.shape[-1]
    window = width // 2 + 1
    columns = width // 2
    channels = spectrum.shape[1]
    hankel_rows = hankel(spectrum, window, columns).reshape(2, channels * window, columns)
    sketch_basis = jnp.einsum('qrp,pk->rqk', hankel_rows, probe, precision=HIGHEST_PRECISION).reshape(channels * window, 2 * probe.shape[1])
    gram_raw = jnp.dot(sketch_basis.T, sketch_basis, precision=HIGHEST_PRECISION)
    cross_raw = jnp.einsum('rk,qrp->qkp', sketch_basis, hankel_rows, precision=HIGHEST_PRECISION)
    gram_matrix, cross_terms = assemble(gram_raw, cross_raw)
    lower_factor = jnp.linalg.cholesky(gram_matrix)
    coeffs = jax.scipy.linalg.cho_solve((lower_factor, True), cross_terms)
    half = coeffs.shape[0] // 2
    real_part = coeffs[:half]
    imag_part = coeffs[half:]
    mixing = jnp.stack([jnp.concatenate([real_part, -imag_part], 0), jnp.concatenate([imag_part, real_part], 0)])
    rebuilt = jnp.einsum('rk,qkp->qrp', sketch_basis, mixing, precision=HIGHEST_PRECISION)
    return diag_mean(rebuilt.reshape(2, channels, window, columns), width)

def reference(traces, probes):
    freq_ids = BAND_LO + jnp.arange(NF, dtype=jnp.int32)
    time_ids = jnp.arange(NT, dtype=jnp.int32)
    forward_table = wave_table(freq_ids, time_ids, NT, NT ** (-0.5))
    spectra = jnp.einsum('qft,tyx->fqyx', forward_table, traces, precision=HIGHEST_PRECISION)
    clean = lax.map(denoise_slice, (spectra, probes))
    inverse_table = wave_table(freq_ids, time_ids, NT, (2.0 / NF) ** 0.5)
    return jnp.einsum('qft,fqyx->tyx', inverse_table, clean, precision=HIGHEST_PRECISION)
```

```python
import functools

import jax
import jax.numpy as jnp
from jax import lax
from jax.experimental import pallas as pl
from jax.experimental.pallas import tpu as pltpu
from jax.sharding import PartitionSpec as P

NT = 1024
BAND_LO = 16
HIGHEST = lax.Precision.HIGHEST
COLORS = 2
AXES = ("freq", "space")


def dot(a, b, contract=(1, 0)):
    return lax.dot_general(
        a,
        b,
        (((contract[0],), (contract[1],)), ((), ())),
        precision=HIGHEST,
        preferred_element_type=jnp.float32,
    )


def log2(n):
    return n.bit_length() - 1


def forward_kernel(who_ref, table_ref, x_ref, send_ref, keep_ref):
    rows = x_ref.shape[-2]
    times = x_ref.shape[0]
    width = x_ref.shape[-1]
    table = table_ref[...]
    half = table.shape[0] // 2
    for g in range(rows // 8):
        x = x_ref[:, 0, 0, g * 8 : g * 8 + 8, :].reshape(times * 8, width)
        y = dot(table, x)
        for ref, part in ((keep_ref, y[:half]), (send_ref, y[half:])):
            ref[:, :, 0, g * 8 : g * 8 + 8, :] = part.reshape(half // 16, 2, 8, width)


def forward(traces, table, who, owners, color):
    times, channels, width = traces.shape
    per = channels // owners // COLORS
    block = min(32, per)
    slices = table.shape[0] // 16
    view = traces.reshape(times, owners, COLORS, per, width)
    out = jax.ShapeDtypeStruct((slices // 2, 2, owners, per, width), jnp.float32)
    out_spec = pl.BlockSpec((slices // 2, 2, 1, block, width), lambda o, j, who: (0, 0, o, j, 0))
    return pl.pallas_call(
        forward_kernel,
        out_shape=(out, out),
        grid_spec=pltpu.PrefetchScalarGridSpec(
            num_scalar_prefetch=1,
            grid=(owners, per // block),
            in_specs=[
                pl.BlockSpec(table.shape, lambda o, j, who: (0, 0)),
                pl.BlockSpec(
                    (times, 1, 1, block, width), lambda o, j, who: (0, o ^ who[0], color, j, 0)
                ),
            ],
            out_specs=(out_spec, out_spec),
        ),
        name="forward",
        cost_estimate=pl.CostEstimate(
            flops=16 * slices * traces.size // COLORS,
            transcendentals=0,
            bytes_accessed=6 * traces.size // COLORS,
        ),
    )(who, table, view)


def inverse_kernel(who_ref, table_ref, *refs):
    out_ref = refs[-1]
    times, _, colors, rows, width = out_ref.shape
    table = table_ref[...]
    for c in range(colors):
        for g in range(rows // 8):
            parts = [
                ref[..., g * 8 : g * 8 + 8, :].reshape(-1, width)
                for ref in refs[2 * c : 2 * c + 2]
            ]
            y = dot(table, jnp.concatenate(parts, 0))
            out_ref[:, 0, c, g * 8 : g * 8 + 8, :] = y.reshape(times, 8, width)


def inverse(pieces, specs, table, who, times, owners, per, width):
    block = min(32, per)
    return pl.pallas_call(
        inverse_kernel,
        out_shape=jax.ShapeDtypeStruct((times, owners, COLORS, per, width), jnp.float32),
        grid_spec=pltpu.PrefetchScalarGridSpec(
            num_scalar_prefetch=1,
            grid=(owners, per // block),
            in_specs=[pl.BlockSpec(table.shape, lambda o, j, who: (0, 0))]
            + [spec(block) for spec in specs],
            out_specs=pl.BlockSpec(
                (times, 1, COLORS, block, width), lambda o, j, who: (0, o ^ who[0], 0, j, 0)
            ),
        ),
        name="inverse",
    )(who, table, *pieces)


def wave(freq_ids, time_ids, factor):
    phase = (freq_ids[:, None] * time_ids[None, :] % NT).astype(jnp.float32) * (2.0 * jnp.pi / NT)
    return jnp.stack([jnp.cos(phase), -jnp.sin(phase)], 1) * factor


def spread(table):
    a, b = table.shape
    eye = jnp.eye(8, dtype=table.dtype)
    return (table[:, None, :, None] * eye[None, :, None, :]).reshape(a * 8, b * 8)


def gather_kernel(a_ref, b_ref, probe_ref, out_ref):
    real = jnp.concatenate([a_ref[0], b_ref[0]], 0)
    imag = jnp.concatenate([a_ref[1], b_ref[1]], 0)
    stacked = jnp.concatenate([real, imag], 0)
    turned = jnp.concatenate([imag, -real], 0)
    probe = probe_ref[...]
    rank = probe.shape[1]
    columns = probe.shape[0]
    for q, other in enumerate((stacked, turned)):
        base = dot(stacked, other, (0, 0))
        total = base
        step = 1
        while step < columns:
            total = total + jnp.roll(total, (-step, -step), (0, 1))
            step *= 2
        hank = total[:columns, :columns] + base[columns:, columns:]
        out_ref[q * rank : (q + 1) * rank, :] = dot(probe, hank, (0, 0))


def solve_kernel(*refs):
    crosses = refs[:-7]
    a_ref, b_ref, probe_ref, out_a, out_b, wr_ref, wi_ref = refs[-7:]
    cross = crosses[0][...]
    for ref in crosses[1:]:
        cross = cross + ref[...]
    probe = probe_ref[...]
    columns, rank = probe.shape
    width = a_ref.shape[-1]
    gram = dot(cross, probe)
    for ref, lo in ((wr_ref, 0), (wi_ref, rank)):
        ref[:, :columns] = jnp.pad(gram[lo : lo + rank], ((0, 0), (0, columns - rank)))
        ref[:, columns:] = cross[lo : lo + rank]
    lane = lax.broadcasted_iota(jnp.int32, (rank, columns), 1)
    lane_row = lax.broadcasted_iota(jnp.int32, (1, columns), 1)

    def step(k, _):
        row_r = wr_ref[pl.ds(k, 1), :]
        row_i = wi_ref[pl.ds(k, 1), :]
        pivot = jnp.sum(jnp.where(lane_row == k, row_r[:, :columns], 0.0), axis=1, keepdims=True)
        inv = 1.0 / pivot
        row_r = row_r * inv
        row_i = row_i * inv
        wr = wr_ref[...]
        wi = wi_ref[...]
        col_r = jnp.sum(jnp.where(lane == k, wr[:, :columns], 0.0), axis=1, keepdims=True)
        col_i = jnp.sum(jnp.where(lane == k, wi[:, :columns], 0.0), axis=1, keepdims=True)
        wr_ref[...] = wr - (col_r * row_r - col_i * row_i)
        wi_ref[...] = wi - (col_r * row_i + col_i * row_r)
        wr_ref[pl.ds(k, 1), :] = row_r
        wi_ref[pl.ds(k, 1), :] = row_i
        return 0

    lax.fori_loop(0, rank, step, 0)
    at = lax.broadcasted_iota(jnp.int32, (1, width), 1)
    counts = jnp.minimum(jnp.minimum(at + 1, width - at), columns).astype(jnp.float32)
    scale = 1.0 / counts
    mix = []
    for ref in (wr_ref, wi_ref):
        g = dot(probe, ref[:, columns:])
        zero = jnp.zeros_like(g)
        total = jnp.concatenate(
            [jnp.concatenate([g, zero], 1), jnp.concatenate([zero, zero], 1)], 0
        )
        last = jnp.concatenate([jnp.concatenate([zero, zero], 1), jnp.concatenate([zero, g], 1)], 0)
        step_size = 1
        while step_size < columns:
            total = total + jnp.roll(total, (step_size, step_size), (0, 1))
            step_size *= 2
        mix.append((total + last) * scale)
    for src, dst in ((a_ref, out_a), (b_ref, out_b)):
        dst[0] = dot(src[0], mix[0]) - dot(src[1], mix[1])
        dst[1] = dot(src[0], mix[1]) + dot(src[1], mix[0])


def combos(bits):
    for d in range(1, 1 << len(bits)):
        on = [(d >> i) & 1 for i in range(len(bits))]
        yield on, sum(o << b for o, b in zip(on, bits))


def body(n_freq, n_space, traces, probes):
    devices = n_freq * n_space
    times, channels, width = traces.shape
    slices = probes.shape[0] * n_freq
    owners = devices // slices
    per = channels // owners // COLORS
    me = lax.axis_index("freq") * n_space + lax.axis_index("space")
    my_slice = me // owners
    my_owner = me % owners

    def swap(x, mask):
        return lax.ppermute(x, AXES, [(i, i ^ mask) for i in range(devices)])

    core = log2(n_space)
    y_bits = list(range(core + 1, log2(devices)))
    sub_bits = list(range(log2(owners), core))
    owner_bits = list(range(log2(owners)))
    x_bits = owner_bits[:1]
    z_bits = owner_bits[1:] + sub_bits
    z_groups = [z_bits[i : i + 2] for i in range(0, len(z_bits), 2)]
    orders = [[x_bits, y_bits] + z_groups, [y_bits, x_bits] + z_groups]

    per_freq = slices // n_freq
    slots = jnp.asarray(
        [
            (y * 2 + c) * per_freq + s
            for c in range(2)
            for y in range(n_freq // 2)
            for s in range(per_freq)
        ],
        jnp.int32,
    )
    freq_ids = BAND_LO + (my_slice ^ slots)
    time_ids = me * times + jnp.arange(times, dtype=jnp.int32)
    table = spread(wave(freq_ids, time_ids, NT ** (-0.5)).reshape(2 * slices, times))
    table_back = spread(
        wave(freq_ids, time_ids, (2.0 / slices) ** 0.5).reshape(2 * slices, times).T
    )
    who = jnp.asarray(my_owner, jnp.int32).reshape(1)

    made = [forward(traces, table, who, owners, c) for c in range(COLORS)]
    pieces = []
    for color in range(COLORS):
        keep, send = made[color][1], made[color][0]
        total = keep + swap(send, 1 << core)
        dims = y_bits[::-1] + sub_bits[::-1] + ["q"] + owner_bits[::-1] + ["c", "x"]
        shape = [2] * (len(dims) - 2) + [per, width]
        pieces.append((total.reshape(shape), dims))

    def pick(x, dims, chosen):
        return x[tuple(chosen.get(d, slice(None)) for d in dims)]

    depth = len(orders[0])
    for stage in range(depth):
        new = []
        for (x, dims), order in zip(pieces, orders):
            bits = order[stage]
            total = pick(x, dims, {b: 0 for b in bits})
            for on, mask in combos(bits):
                total = total + swap(pick(x, dims, dict(zip(bits, on))), mask)
            new.append((total, [d for d in dims if d not in bits]))
        pieces = new
    spectra = [x for x, _ in pieces]

    sub = my_slice - lax.axis_index("freq") * per_freq
    probe = lax.dynamic_index_in_dim(probes, sub, 0, keepdims=False)
    rank = probe.shape[1]
    columns = probe.shape[0]
    cross = pl.pallas_call(
        gather_kernel,
        out_shape=jax.ShapeDtypeStruct((2 * rank, columns), jnp.float32),
        name="gather",
    )(*spectra, probe)
    crosses = [cross] + [swap(cross, mask) for _, mask in combos(owner_bits)]
    clean = pl.pallas_call(
        solve_kernel,
        out_shape=[jax.ShapeDtypeStruct(spectra[0].shape, jnp.float32)] * 2,
        scratch_shapes=[pltpu.VMEM((rank, 2 * columns), jnp.float32)] * 2,
        name="solve",
    )(*crosses, *spectra, probe)

    held = [(x, ["q", "c", "x"]) for x in clean]
    for stage in reversed(range(depth)):
        new = []
        for (x, dims), order in zip(held, orders):
            bits = order[stage]
            parts = [x] + [swap(x, mask) for _, mask in combos(bits)]
            stacked = jnp.stack(parts).reshape([2] * len(bits) + list(x.shape))
            new.append((stacked, bits[::-1] + dims))
        held = new
    finals, specs = [], []
    for x, dims in held:
        finals += [x, swap(x, 1 << core)]

        def spec(block, dims=dims):
            shape = [
                block if d == "c" else width if d == "x" else 1 if d in owner_bits else 2
                for d in dims
            ]

            def index(o, j, who):
                return tuple(
                    j if d == "c" else (o >> d) & 1 if d in owner_bits else 0 for d in dims
                )

            return pl.BlockSpec(tuple(shape), index)

        specs += [spec, spec]
    for _, dims in held:
        order = [d for d in dims if d in y_bits or d in sub_bits]
        assert order == y_bits[::-1] + sub_bits[::-1]
    out = inverse(finals, specs, table_back, who, times, owners, per, width)
    return out.reshape(times, channels, width)


def solution(mesh):
    n_freq, n_space = mesh.shape["freq"], mesh.shape["space"]
    in_specs = (P(AXES, None, None), P("freq", None, None))
    return jax.shard_map(
        functools.partial(body, n_freq, n_space),
        mesh=mesh,
        in_specs=in_specs,
        out_specs=P(AXES, None, None),
        check_vma=False,
    )
```

```python
import functools

import jax
import jax.numpy as jnp
from jax import lax
from jax.experimental import pallas as pl
from jax.experimental.pallas import tpu as pltpu
from jax.sharding import PartitionSpec as P

NT = 1024
BAND_LO = 16
HIGHEST = lax.Precision.HIGHEST
COLORS = 2
PAIRS = 2
AXES = ("freq", "space")


def dot(a, b, contract=(1, 0)):
    return lax.dot_general(
        a,
        b,
        (((contract[0],), (contract[1],)), ((), ())),
        precision=HIGHEST,
        preferred_element_type=jnp.float32,
    )


def dot16(a, b):
    return lax.dot_general(a, b, (((1,), (0,)), ((), ())), preferred_element_type=jnp.float32)


def split(x, parts):
    out = []
    for i in range(parts):
        part = x.astype(jnp.bfloat16)
        out.append(part)
        if i + 1 < parts:
            x = x - part.astype(jnp.float32)
    return out


def log2(n):
    return n.bit_length() - 1


def forward_kernel(who_ref, table_ref, x_ref, send_ref, keep_ref, parts_ref):
    times, colors, rows, width = x_ref.shape[0], *x_ref.shape[-3:]
    size = table_ref.shape[0]
    half = size // 2

    @pl.when(pl.program_id(0) == 0)
    def _():
        for i, part in enumerate(split(table_ref[...], 3)):
            parts_ref[i * size : (i + 1) * size, :] = part

    for c in range(colors):
        for g in range(rows // 8):
            x = x_ref[:, 0, 0, c, g * 8 : g * 8 + 8, :].reshape(times * 8, width)
            high, mid, low = split(x, 3)
            a = dot16(parts_ref[...], high)
            b = dot16(parts_ref[: 2 * size, :], mid)
            d = dot16(parts_ref[:size, :], low)
            y = a[:size] + (a[size : 2 * size] + b[:size]) + (a[2 * size :] + b[size:] + d)
            for ref, part in ((keep_ref, y[:half]), (send_ref, y[half:])):
                ref[:, :, 0, c, g * 8 : g * 8 + 8, :] = part.reshape(half // 16, 2, 8, width)


def forward(traces, table, who, owners, pair):
    times, channels, width = traces.shape
    per = channels // owners // COLORS // PAIRS
    slices = table.shape[0] // 16
    view = traces.reshape(times, owners, PAIRS, COLORS, per, width)
    out = jax.ShapeDtypeStruct((slices // 2, 2, owners, COLORS, per, width), jnp.float32)
    out_spec = pl.BlockSpec(
        (slices // 2, 2, 1, COLORS, per, width), lambda o, who: (0, 0, o, 0, 0, 0)
    )
    return pl.pallas_call(
        forward_kernel,
        out_shape=(out, out),
        grid_spec=pltpu.PrefetchScalarGridSpec(
            num_scalar_prefetch=1,
            grid=(owners,),
            in_specs=[
                pl.BlockSpec(table.shape, lambda o, who: (0, 0)),
                pl.BlockSpec(
                    (times, 1, 1, COLORS, per, width), lambda o, who: (0, o ^ who[0], pair, 0, 0, 0)
                ),
            ],
            out_specs=(out_spec, out_spec),
            scratch_shapes=[pltpu.VMEM((3 * table.shape[0], table.shape[1]), jnp.bfloat16)],
        ),
        name="forward",
        cost_estimate=pl.CostEstimate(
            flops=128 * slices * traces.size // PAIRS,
            transcendentals=0,
            bytes_accessed=6 * traces.size // PAIRS,
        ),
    )(who, table, view)


def inverse_kernel(who_ref, table_ref, here_ref, there_ref, *refs):
    out_ref, parts_ref = refs[-2:]
    times, colors, rows, width = out_ref.shape[0], *out_ref.shape[-3:]
    size = table_ref.shape[0]

    @pl.when(pl.program_id(0) == 0)
    def _():
        for i, part in enumerate(split(table_ref[...], 2)):
            parts_ref[i * size : (i + 1) * size, :] = part

    for c in range(colors):
        for g in range(rows // 8):
            parts = [
                ref[0, :, :, c, g * 8 : g * 8 + 8, :].reshape(-1, width)
                for ref in (here_ref, there_ref)
            ]
            high, low = split(jnp.concatenate(parts, 0), 2)
            a = dot16(parts_ref[...], high)
            y = a[:size] + (a[size:] + dot16(parts_ref[:size, :], low))
            out_ref[:, 0, 0, c, g * 8 : g * 8 + 8, :] = y.reshape(times, 8, width)


def inverse(here, there, table, who, times, pair, before):
    owners, half, _, _, per, width = here.shape
    block = pl.BlockSpec((1, half, 2, COLORS, per, width), lambda o, who: (o, 0, 0, 0, 0, 0))
    extra = [] if before is None else [before]
    return pl.pallas_call(
        inverse_kernel,
        out_shape=jax.ShapeDtypeStruct((times, owners, PAIRS, COLORS, per, width), jnp.float32),
        grid_spec=pltpu.PrefetchScalarGridSpec(
            num_scalar_prefetch=1,
            grid=(owners,),
            in_specs=[pl.BlockSpec(table.shape, lambda o, who: (0, 0)), block, block]
            + [pl.BlockSpec(memory_space=pl.ANY)] * len(extra),
            out_specs=pl.BlockSpec(
                (times, 1, 1, COLORS, per, width), lambda o, who: (0, o ^ who[0], pair, 0, 0, 0)
            ),
            scratch_shapes=[pltpu.VMEM((2 * table.shape[0], table.shape[1]), jnp.bfloat16)],
        ),
        input_output_aliases={4: 0} if extra else {},
        name="inverse",
        cost_estimate=pl.CostEstimate(
            flops=64 * half * times * here.size // half,
            transcendentals=0,
            bytes_accessed=16 * here.size,
        ),
    )(who, table, here, there, *extra)


def wave(freq_ids, time_ids, factor):
    phase = (freq_ids[:, None] * time_ids[None, :] % NT).astype(jnp.float32) * (2.0 * jnp.pi / NT)
    return jnp.stack([jnp.cos(phase), -jnp.sin(phase)], 1) * factor


def spread(table):
    a, b = table.shape
    eye = jnp.eye(8, dtype=table.dtype)
    return (table[:, None, :, None] * eye[None, :, None, :]).reshape(a * 8, b * 8)


def gather_kernel(*refs):
    *spectra, probe_ref, out_ref = refs
    width = spectra[0].shape[-1]
    real = jnp.concatenate([ref[:, 0].reshape(-1, width) for ref in spectra], 0)
    imag = jnp.concatenate([ref[:, 1].reshape(-1, width) for ref in spectra], 0)
    stacked = jnp.concatenate([real, imag], 0)
    turned = jnp.concatenate([imag, -real], 0)
    probe = probe_ref[...]
    rank = probe.shape[1]
    columns = probe.shape[0]
    for q, other in enumerate((stacked, turned)):
        base = dot(stacked, other, (0, 0))
        total = base
        step = 1
        while step < columns:
            total = total + jnp.roll(total, (-step, -step), (0, 1))
            step *= 2
        hank = total[:columns, :columns] + base[columns:, columns:]
        out_ref[q * rank : (q + 1) * rank, :] = dot(probe, hank, (0, 0))


def solve_kernel(*refs):
    *crosses, probe_ref, out_ref, wr_ref, wi_ref = refs
    cross = crosses[0][...]
    for ref in crosses[1:]:
        cross = cross + ref[...]
    probe = probe_ref[...]
    columns, rank = probe.shape
    gram = dot(cross, probe)
    for ref, lo in ((wr_ref, 0), (wi_ref, rank)):
        ref[:, :columns] = jnp.pad(gram[lo : lo + rank], ((0, 0), (0, columns - rank)))
        ref[:, columns:] = cross[lo : lo + rank]
    lane = lax.broadcasted_iota(jnp.int32, (rank, columns), 1)
    lane_row = lax.broadcasted_iota(jnp.int32, (1, columns), 1)

    def step(k, _):
        row_r = wr_ref[pl.ds(k, 1), :]
        row_i = wi_ref[pl.ds(k, 1), :]
        pivot = jnp.sum(jnp.where(lane_row == k, row_r[:, :columns], 0.0), axis=1, keepdims=True)
        inv = 1.0 / pivot
        row_r = row_r * inv
        row_i = row_i * inv
        wr = wr_ref[...]
        wi = wi_ref[...]
        col_r = jnp.sum(jnp.where(lane == k, wr[:, :columns], 0.0), axis=1, keepdims=True)
        col_i = jnp.sum(jnp.where(lane == k, wi[:, :columns], 0.0), axis=1, keepdims=True)
        wr_ref[...] = wr - (col_r * row_r - col_i * row_i)
        wi_ref[...] = wi - (col_r * row_i + col_i * row_r)
        wr_ref[pl.ds(k, 1), :] = row_r
        wi_ref[pl.ds(k, 1), :] = row_i
        return 0

    lax.fori_loop(0, rank, step, 0)
    out_ref[:rank, :] = wr_ref[:, columns:]
    out_ref[rank:, :] = wi_ref[:, columns:]


def mix_kernel(width, slots, *refs):
    *coeffs, probe_ref, high_ref, low_ref = refs
    columns, rank = probe_ref.shape[1:]
    at = lax.broadcasted_iota(jnp.int32, (1, width), 1)
    counts = jnp.minimum(jnp.minimum(at + 1, width - at), columns).astype(jnp.float32)
    scale = 1.0 / counts
    for s in range(slots):
        probe = probe_ref[s]
        for q in range(2):
            g = dot(probe, coeffs[s][q * rank : (q + 1) * rank, :])
            zero = jnp.zeros_like(g)
            above = jnp.concatenate([g, zero], 1)
            below = jnp.concatenate([zero, g], 1)
            none = jnp.zeros_like(above)
            total = jnp.concatenate([above, none], 0)
            step = 1
            while step < columns:
                total = total + jnp.roll(total, (step, step), (0, 1))
                step *= 2
            m = (total + jnp.concatenate([none, below], 0)) * scale
            high_ref[s, q], low_ref[s, q] = split(m, 2)


def clean_kernel(n_a, n_b, *refs):
    a_refs, b_refs = refs[:n_a], refs[n_a : n_a + n_b]
    high_ref, low_ref, out_ref = refs[n_a + n_b :]
    n_y, n_sub, n_rest, _, per, width = a_refs[0].shape
    n_x = b_refs[0].shape[0]
    for y in range(n_y):
        for s in range(n_sub):
            slot = y * n_sub + s
            place = [(r * n_x + x, c) for r in range(n_rest) for x in range(n_x) for c in range(2)]
            blocks = []
            for q in range(2):
                for o, c in place:
                    x, r = o % n_x, o // n_x
                    blocks.append(a_refs[x][y, s, r, q] if c == 0 else b_refs[y][x, s, r, q])
            high, low = split(jnp.concatenate(blocks, 0), 2)
            half = high.shape[0] // 2
            by = []
            for q in range(2):
                m = high_ref[slot, q]
                by.append(dot16(high, m) + (dot16(low, m) + dot16(high, low_ref[slot, q])))
            real = by[0][:half] - by[1][half:]
            imag = by[0][half:] + by[1][:half]
            for i, (o, c) in enumerate(place):
                out_ref[o, slot, 0, c] = real[i * per : (i + 1) * per]
                out_ref[o, slot, 1, c] = imag[i * per : (i + 1) * per]


def combos(bits):
    for d in range(1, 1 << len(bits)):
        on = [(d >> i) & 1 for i in range(len(bits))]
        yield on, sum(o << b for o, b in zip(on, bits))


def body(n_freq, n_space, traces, probes):
    devices = n_freq * n_space
    times, channels, width = traces.shape
    slices = probes.shape[0] * n_freq
    per_freq = slices // n_freq
    owners = devices // slices
    per = channels // owners // COLORS // PAIRS
    me = lax.axis_index("freq") * n_space + lax.axis_index("space")
    my_slice = me // owners
    my_owner = me % owners

    def swap(x, mask):
        return lax.ppermute(x, AXES, [(i, i ^ mask) for i in range(devices)])

    core = log2(n_space)
    y_bits = list(range(core + 1, log2(devices)))
    sub_bits = list(range(log2(owners), core))
    owner_bits = list(range(log2(owners)))
    x_bits = owner_bits[:1]
    z_bits = owner_bits[1:] + sub_bits
    orders = [[x_bits, y_bits], [y_bits, x_bits]]
    n_y, n_sub, n_x, n_rest = n_freq // 2, per_freq, 2, owners // 2

    slots = jnp.asarray(
        [(y * 2 + c) * n_sub + s for c in range(2) for y in range(n_y) for s in range(n_sub)],
        jnp.int32,
    )
    freq_ids = BAND_LO + (my_slice ^ slots)
    time_ids = me * times + jnp.arange(times, dtype=jnp.int32)
    table = spread(wave(freq_ids, time_ids, NT ** (-0.5)).reshape(2 * slices, times))
    table_back = spread(
        wave(freq_ids, time_ids, (2.0 / slices) ** 0.5).reshape(2 * slices, times).T
    )
    who = jnp.asarray(my_owner, jnp.int32).reshape(1)

    sub = my_slice - lax.axis_index("freq") * per_freq
    own_probes = jnp.stack(
        [lax.dynamic_index_in_dim(probes, sub ^ s, 0, keepdims=False) for s in range(n_sub)]
    )
    all_probes = jnp.concatenate([own_probes] + [swap(own_probes, m) for _, m in combos(y_bits)])
    probe = own_probes[0]
    columns, rank = probe.shape

    dims = y_bits[::-1] + sub_bits[::-1] + ["q"] + owner_bits[::-1] + ["color", "c", "x"]
    shape = [2] * (len(dims) - 2) + [per, width]

    def pick(x, dims, chosen):
        return x[tuple(chosen.get(d, slice(None)) for d in dims)]

    def add(terms):
        return functools.reduce(lambda a, b: a + b, terms)

    made = [forward(traces, table, who, owners, p) for p in range(PAIRS)]
    spectra = []
    for send, keep in made:
        terms = [keep.reshape(shape), swap(send, 1 << core).reshape(shape)]
        ends = []
        for color, order in enumerate(orders):
            mine = [pick(t, dims, {"color": color}) for t in terms]
            left = [d for d in dims if d != "color"]
            for bits in order:
                came = [
                    swap(add([pick(t, left, dict(zip(bits, on))) for t in mine]), mask)
                    for on, mask in combos(bits)
                ]
                mine = [pick(t, left, {b: 0 for b in bits}) for t in mine] + came
                left = [d for d in left if d not in bits]
            ends.append((mine, left))

        def both(on):
            return jnp.stack(
                [add([pick(t, left, dict(zip(z_bits, on))) for t in mine]) for mine, left in ends]
            )

        total = both([0] * len(z_bits))
        spectra.append(add([total] + [swap(both(on), mask) for on, mask in combos(z_bits)]))

    cross = pl.pallas_call(
        gather_kernel,
        out_shape=jax.ShapeDtypeStruct((2 * rank, columns), jnp.float32),
        name="gather",
    )(*spectra, probe)
    crosses = [cross] + [swap(cross, mask) for _, mask in combos(owner_bits)]
    coeffs = pl.pallas_call(
        solve_kernel,
        out_shape=jax.ShapeDtypeStruct((2 * rank, columns), jnp.float32),
        scratch_shapes=[pltpu.VMEM((rank, 2 * columns), jnp.float32)] * 2,
        name="solve",
        cost_estimate=pl.CostEstimate(flops=1 << 27, transcendentals=0, bytes_accessed=1 << 18),
    )(*crosses, probe)
    all_coeffs = [coeffs] + [swap(coeffs, mask) for _, mask in combos(sub_bits + y_bits)]
    mixes = pl.pallas_call(
        functools.partial(mix_kernel, width, n_y * n_sub),
        out_shape=[jax.ShapeDtypeStruct((n_y * n_sub, 2, width, width), jnp.bfloat16)] * 2,
        name="mix",
    )(*all_coeffs, all_probes)

    out = None
    for p, s in enumerate(spectra):
        parts = [s] + [swap(s, mask) for _, mask in combos(z_bits)]
        args = []
        for color, order in enumerate(orders):
            held = jnp.stack([t[color] for t in parts])
            last, first = order
            held = jnp.stack([held] + [swap(held, mask) for _, mask in combos(first)])
            n_first = held.shape[0]
            ends = [held] + [swap(held, mask) for _, mask in combos(last)]
            args += [e.reshape(n_first, n_sub, n_rest, 2, per, width) for e in ends]
        clean = pl.pallas_call(
            functools.partial(clean_kernel, n_x, n_y),
            out_shape=jax.ShapeDtypeStruct(
                (owners, n_y * n_sub, 2, COLORS, per, width), jnp.float32
            ),
            name="clean",
        )(*args, *mixes)
        other = swap(clean, 1 << core)
        out = inverse(clean, other, table_back, who, times, p, out)
    return out.reshape(times, channels, width)


def solution(mesh):
    n_freq, n_space = mesh.shape["freq"], mesh.shape["space"]
    in_specs = (P(AXES, None, None), P("freq", None, None))
    return jax.shard_map(
        functools.partial(body, n_freq, n_space),
        mesh=mesh,
        in_specs=in_specs,
        out_specs=P(AXES, None, None),
        check_vma=False,
    )
```
